512 devices in a mesh: row: 16 (over z), col: 32 (over x, y, core).
Axes of the slice: x: 4, y: 4, z: 16, core: 2. Of those that a mesh axis runs over, the one named last changes fastest.
Arguments:
- matrix: float32 [8, 16, 128, 4, 32, 128], P(None, 'row', None, None, 'col'), as said below
Outputs:
- reduced: float32 [8, 16, 128, 4, 32, 128], P(None, 'row', None, None, 'col')
Inputs may be any that keep to these rules, and one draw needn't show every extreme that they name: matrix is exactly symmetric as an 16384 x 16384 matrix.
All inputs are finite; a program needn't handle non-finite values.
Results may differ from the reference program's by a relative error of at most 0.00016.
Values sent between devices are 32-bit elements; how exact they have to be, the bound alone decides.
No kernel may reach another device: no remote copies, remote signals or barrier semaphores. Data moves between devices by JAX's collectives and lax.ppermute only.
A program may use at most 64 MiB of HBM per device.

```python
import jax
import jax.numpy as jnp
from jax import lax

ORDER = 16384
BLOCK = 128
N_ROW = 16
N_COL = 32


def draw_matrix(key, part):
    first_key, second_key = jax.random.split(jax.random.fold_in(key, 7), 2)
    noise = jax.random.normal(first_key, (ORDER, ORDER), jnp.float32)
    symmetric = (noise + noise.T) * 0.7071
    owners = (jnp.arange(ORDER) // BLOCK % N_ROW).astype(jnp.float32)
    rising = 3.0 ** (owners / max(N_ROW - 1, 1))
    base = jnp.exp(jax.random.uniform(second_key, (ORDER,), jnp.float32, jnp.log(0.5), jnp.log(2.0)))
    scales = base * rising * 0.577
    outer = scales[:, None] * scales[None, :]
    result = symmetric * outer
    return result.reshape(ORDER // BLOCK // N_ROW, N_ROW, BLOCK, ORDER // BLOCK // N_COL, N_COL, BLOCK)


def setup_inputs(seed: int = 0) -> dict:
    seeds = jax.random.split(jax.random.key(seed), 2)
    return {
        "matrix": draw_matrix(jax.random.fold_in(seeds[1], 71), 0),
    }


newton_sweeps = 8

def product_of(left_side, right_side):
    return jnp.dot(left_side.astype(jnp.float32), right_side.astype(jnp.float32), precision=lax.Precision.HIGHEST, preferred_element_type=jnp.float32)

def newton_inverse(middle):
    identity = jnp.eye(middle.shape[0], dtype=jnp.float32)
    approx = identity
    for sweep_step in range(newton_sweeps):
        approx = product_of(approx, 2.0 * identity - product_of(middle, approx))
    return approx

def panel_step(whole_matrix, panel_index):
    first_row = (panel_index + 1) * BLOCK
    row_ids = jnp.arange(ORDER, dtype=jnp.int32)
    column = whole_matrix[:, panel_index * BLOCK:(panel_index + 1) * BLOCK]
    panel_rows = jnp.where((row_ids >= first_row)[:, None], column, jnp.zeros_like(column))
    gram_matrix = product_of(panel_rows.T, panel_rows)
    lower_factor = jnp.linalg.cholesky(gram_matrix)
    orthonormal = lax.linalg.triangular_solve(lower_factor, panel_rows, left_side=False, lower=True, transpose_a=True)
    identity = jnp.eye(BLOCK, dtype=jnp.float32)
    top_block = orthonormal[first_row:first_row + BLOCK]
    inverse_core = newton_inverse(identity + top_block)
    reflectors = orthonormal.at[first_row:first_row + BLOCK].add(identity)
    products = product_of(whole_matrix, reflectors)
    cross_gram = product_of(reflectors.T, products)
    core_block = product_of(product_of(inverse_core, cross_gram), inverse_core.T)
    companion = product_of(products, inverse_core.T) - 0.5 * product_of(reflectors, core_block)
    left_factor = jnp.concatenate([reflectors, companion], axis=1)
    right_factor = jnp.concatenate([companion, reflectors], axis=1)
    return whole_matrix - product_of(left_factor, right_factor.T)

def reference(matrix):
    whole_matrix = matrix.reshape(ORDER, ORDER)
    whole_matrix = panel_step(whole_matrix, 0)
    whole_matrix = panel_step(whole_matrix, 1)
    return whole_matrix.reshape(matrix.shape)
```

```python
import jax
import jax.numpy as jnp
from jax import lax
from jax.sharding import PartitionSpec as P

newton_sweeps = 8


def dot(left_side, right_side, left_dim=1, right_dim=0):
    return lax.dot_general(
        left_side,
        right_side,
        (((left_dim,), (right_dim,)), ((), ())),
        precision=lax.Precision.HIGHEST,
        preferred_element_type=jnp.float32,
    )


def newton_inverse(middle):
    identity = jnp.eye(middle.shape[0], dtype=jnp.float32)
    power = identity - middle
    approx = identity + power
    for sweep_step in range(1, newton_sweeps):
        power = dot(power, power)
        approx = approx + dot(approx, power)
    return approx


def exchange(chunks, axis):
    return lax.all_to_all(chunks, axis, 0, 0)


def spread_chunk(chunk, axis, count):
    return exchange(jnp.broadcast_to(chunk[None], (count,) + chunk.shape), axis)


def panel_core(gram_and_top, block):
    gram = gram_and_top[:block]
    top = gram_and_top[block:]
    identity = jnp.eye(block, dtype=jnp.float32)
    lower = jnp.linalg.cholesky(gram)
    lower_inverse = lax.linalg.triangular_solve(lower, identity, left_side=True, lower=True)
    top_q = dot(top, lower_inverse, 1, 1)
    pivot_tile = identity + top_q
    return lower_inverse, pivot_tile, newton_inverse(pivot_tile)


def local(matrix):
    tile_rows, block, tile_cols = matrix.shape[0], matrix.shape[2], matrix.shape[3]
    rows, cols = tile_rows * block, tile_cols * block
    row_count, col_count = lax.axis_size("row"), lax.axis_size("col")
    row_index, col_index = lax.axis_index("row"), lax.axis_index("col")
    row_tiles = jnp.repeat(jnp.arange(tile_rows, dtype=jnp.int32) * row_count + row_index, block)[:, None]
    col_tiles = jnp.repeat(jnp.arange(tile_cols, dtype=jnp.int32) * col_count + col_index, block)[:, None]
    row_chunk, col_chunk = rows // col_count, cols // row_count
    small = 2 * block // col_count
    identity = jnp.eye(block, dtype=jnp.float32)

    def below(values, tiles, first):
        return jnp.where(tiles >= first, values, 0.0)

    def with_pivot(values, tiles, pivot):
        shape = (values.shape[0] // block, block, block)
        lifted = jnp.broadcast_to(identity[None], shape).reshape(values.shape)
        return values + jnp.where(tiles == pivot, lifted, 0.0)

    current = matrix.reshape(rows, cols)

    own_col = current[:, :block]
    masked = below(own_col, row_tiles, 1)
    gram_part = dot(masked, masked, 0, 0)
    top_part = jnp.where(row_index == 1 % row_count, own_col[:block], 0.0)
    stacked = jnp.concatenate([gram_part, top_part]).reshape(col_count, small, block)
    got = exchange(jnp.concatenate([own_col.reshape(col_count, row_chunk, block), stacked], axis=1), "col")
    panel_chunk, next_chunk, small_chunk = got[0, :row_chunk], got[1, :row_chunk], got[0, row_chunk:]

    own_row = current[:block].T.reshape(row_count, col_chunk, block)
    copies = jnp.broadcast_to(small_chunk[None], (row_count, small, block))
    got = exchange(jnp.concatenate([own_row, copies], axis=1), "row")
    col_pieces = spread_chunk(got[:2, :col_chunk], "row", row_count)
    small_sum = got[:, col_chunk:].sum(0)
    got = spread_chunk(jnp.concatenate([panel_chunk, small_sum]), "col", col_count)
    panel_rows = got[:, :row_chunk].reshape(rows, block)
    gram_and_top = got[:, row_chunk:].reshape(2 * block, block)
    next_rows = spread_chunk(next_chunk, "col", col_count).reshape(rows, block)
    col_pieces, next_rows = lax.optimization_barrier((col_pieces, next_rows))
    panel_cols = col_pieces[:, 0].reshape(cols, block)
    next_cols = col_pieces[:, 1].reshape(cols, block)

    for panel_index in range(2):
        last = panel_index == 1
        first = panel_index + 1
        lower_inverse, pivot_tile, inverse_core = panel_core(gram_and_top, block)
        reflect_rows = with_pivot(dot(below(panel_rows, row_tiles, first), lower_inverse, 1, 1), row_tiles, first)
        reflect_cols = with_pivot(dot(below(panel_cols, col_tiles, first), lower_inverse, 1, 1), col_tiles, first)

        part_rows = dot(current, reflect_cols)
        part_cols = dot(current, reflect_rows, 0, 0).reshape(row_count, col_chunk, block)
        pieces = [dot(reflect_rows, part_rows, 0, 0)]
        if last:
            pieces.append(jnp.zeros_like(pieces[0]))
        else:
            pieces.append(jnp.where(row_index == first % row_count, part_rows[:block], 0.0))
        stacked = jnp.concatenate(pieces).reshape(col_count, small, block)
        got = exchange(jnp.concatenate([part_rows.reshape(col_count, row_chunk, block), stacked], axis=1), "col").sum(0)
        w_chunk, small_chunk = got[:row_chunk], got[row_chunk:]
        copies = jnp.broadcast_to(small_chunk[None], (row_count, small, block))
        got = exchange(jnp.concatenate([part_cols, copies], axis=1), "row").sum(0)
        w_cols = spread_chunk(got[:col_chunk], "row", row_count).reshape(cols, block)
        got = spread_chunk(jnp.concatenate([w_chunk, got[col_chunk:]]), "col", col_count)
        w_rows = got[:, :row_chunk].reshape(rows, block)
        stacked = got[:, row_chunk:].reshape(small * col_count, block)

        core_block = dot(dot(inverse_core, stacked[:block]), inverse_core, 1, 1)
        companion_rows = dot(w_rows, inverse_core, 1, 1) - 0.5 * dot(reflect_rows, core_block)
        companion_cols = dot(w_cols, inverse_core, 1, 1) - 0.5 * dot(reflect_cols, core_block)
        if not last:
            companion_tile = dot(stacked[block:], inverse_core, 1, 1) - 0.5 * dot(pivot_tile, core_block)
            tile_factor = jnp.concatenate([companion_tile, pivot_tile], axis=1)
            panel_cols = next_cols - dot(jnp.concatenate([reflect_cols, companion_cols], axis=1), tile_factor, 1, 1)
            masked = below(panel_cols, col_tiles, first + 1)
            gram_part = dot(masked, masked, 0, 0)
            top_part = jnp.where(col_index == (first + 1) % col_count, panel_cols[:block], 0.0)
            stacked = jnp.concatenate([gram_part, top_part]).reshape(col_count, small, block)
            small_sum = exchange(stacked, "col").sum(0)
            gram_and_top = spread_chunk(small_sum, "col", col_count).reshape(2 * block, block)
            panel_rows = next_rows - dot(jnp.concatenate([reflect_rows, companion_rows], axis=1), tile_factor, 1, 1)
        left_factor = jnp.concatenate([reflect_rows, companion_rows], axis=1)
        right_factor = jnp.concatenate([companion_cols, reflect_cols], axis=1)
        current = current - dot(left_factor, right_factor, 1, 1)
    return current.reshape(matrix.shape)


def solution(mesh):
    in_specs = (P(None, "row", None, None, "col", None),)
    out_specs = P(None, "row", None, None, "col", None)
    return jax.shard_map(local, mesh=mesh, in_specs=in_specs, out_specs=out_specs, check_vma=False)
```

```python
import jax
import jax.numpy as jnp
from jax import lax
from jax.sharding import PartitionSpec as P

newton_sweeps = 8


def dot(left_side, right_side, left_dim=1, right_dim=0):
    return lax.dot_general(
        left_side,
        right_side,
        (((left_dim,), (right_dim,)), ((), ())),
        precision=lax.Precision.HIGHEST,
        preferred_element_type=jnp.float32,
    )


def newton_inverse(middle):
    identity = jnp.eye(middle.shape[0], dtype=jnp.float32)
    power = identity - middle
    approx = identity + power
    for sweep_step in range(1, newton_sweeps):
        power = dot(power, power)
        approx = approx + dot(approx, power)
    return approx


def exchange(chunks, axis):
    return lax.all_to_all(chunks, axis, 0, 0)


def panel_core(gram_and_top, block):
    gram = gram_and_top[:block]
    top = gram_and_top[block:]
    identity = jnp.eye(block, dtype=jnp.float32)
    lower = jnp.linalg.cholesky(gram)
    lower_inverse = lax.linalg.triangular_solve(lower, identity, left_side=True, lower=True)
    top_q = dot(top, lower_inverse, 1, 1)
    pivot_tile = identity + top_q
    return lower_inverse, pivot_tile, newton_inverse(pivot_tile)


def local(matrix):
    tile_rows, block, tile_cols = matrix.shape[0], matrix.shape[2], matrix.shape[3]
    rows, cols = tile_rows * block, tile_cols * block
    row_count, col_count = lax.axis_size("row"), lax.axis_size("col")
    row_index, col_index = lax.axis_index("row"), lax.axis_index("col")
    spread = col_count // row_count
    part = cols // col_count
    chunk = spread * part
    small = 2 * block // col_count

    row_tiles = jnp.repeat(jnp.arange(tile_rows, dtype=jnp.int32) * row_count + row_index, block)[:, None]
    col_tiles = jnp.repeat(jnp.arange(tile_cols, dtype=jnp.int32) * col_count + col_index, block)[:, None]
    identity = jnp.eye(block, dtype=jnp.float32)

    def below(values, tiles, first):
        return jnp.where(tiles >= first, values, 0.0)

    def with_pivot(values, tiles, pivot):
        shape = (values.shape[0] // block, block, block)
        lifted = jnp.broadcast_to(identity[None], shape).reshape(values.shape)
        return values + jnp.where(tiles == pivot, lifted, 0.0)

    def chunks_of(values):
        split = values.reshape(tile_cols, spread, block // part, part, block)
        return split.transpose(0, 2, 1, 3, 4).reshape(col_count, chunk, block)

    def rows_of(chunks):
        split = chunks.reshape(tile_cols, block // part, spread, part, block)
        return split.transpose(0, 2, 1, 3, 4).reshape(rows, block)

    def share(tall, stacked):
        mine = jnp.concatenate(tall + [stacked])
        got = exchange(jnp.broadcast_to(mine[None], (row_count,) + mine.shape), "row")
        sends = []
        for index, piece in enumerate(tall):
            sends.append(jnp.broadcast_to(piece[None], (col_count, chunk, block)))
            wanted = got[:, index * chunk : (index + 1) * chunk].reshape(row_count, spread, part, block)
            sends.append(wanted.transpose(1, 0, 2, 3).reshape(col_count, part, block))
        total = got[:, len(tall) * chunk :].sum(0)
        sends.append(jnp.broadcast_to(total[None], (col_count,) + total.shape))
        got = exchange(jnp.concatenate(sends, axis=1), "col")
        results = []
        for index in range(len(tall)):
            start = index * (chunk + part)
            results.append(rows_of(got[:, start : start + chunk]))
            results.append(got[:, start + chunk : start + chunk + part].reshape(cols, block))
        results.append(got[:, len(tall) * (chunk + part) :].reshape(col_count * small, block))
        return results

    current = matrix.reshape(rows, cols)

    own_col = current[:, :block]
    masked = below(own_col, row_tiles, 1)
    gram_part = dot(masked, masked, 0, 0)
    top_part = jnp.where(row_index == 1 % row_count, own_col[:block], 0.0)
    stacked = jnp.concatenate([gram_part, top_part]).reshape(col_count, small, block)
    got = exchange(jnp.concatenate([chunks_of(own_col), stacked], axis=1), "col")
    panel_rows, panel_cols, next_rows, next_cols, gram_and_top = share(
        [got[0, :chunk], got[1, :chunk]], got[0, chunk:]
    )

    for panel_index in range(2):
        last = panel_index == 1
        first = panel_index + 1
        lower_inverse, pivot_tile, inverse_core = panel_core(gram_and_top, block)
        reflect_rows = with_pivot(dot(below(panel_rows, row_tiles, first), lower_inverse, 1, 1), row_tiles, first)
        reflect_cols = with_pivot(dot(below(panel_cols, col_tiles, first), lower_inverse, 1, 1), col_tiles, first)

        part_rows = dot(current, reflect_cols)
        pieces = [dot(reflect_rows, part_rows, 0, 0)]
        if last:
            pieces.append(jnp.zeros_like(pieces[0]))
        else:
            pieces.append(jnp.where(row_index == first % row_count, part_rows[:block], 0.0))
        stacked = jnp.concatenate(pieces).reshape(col_count, small, block)
        got = exchange(jnp.concatenate([chunks_of(part_rows), stacked], axis=1), "col").sum(0)
        w_rows, w_cols, stacked = share([got[:chunk]], got[chunk:])

        core_block = dot(dot(inverse_core, stacked[:block]), inverse_core, 1, 1)
        companion_rows = dot(w_rows, inverse_core, 1, 1) - 0.5 * dot(reflect_rows, core_block)
        companion_cols = dot(w_cols, inverse_core, 1, 1) - 0.5 * dot(reflect_cols, core_block)
        if not last:
            companion_tile = dot(stacked[block:], inverse_core, 1, 1) - 0.5 * dot(pivot_tile, core_block)
            tile_factor = jnp.concatenate([companion_tile, pivot_tile], axis=1)
            panel_cols = next_cols - dot(jnp.concatenate([reflect_cols, companion_cols], axis=1), tile_factor, 1, 1)
            masked = below(panel_cols, col_tiles, first + 1)
            gram_part = dot(masked, masked, 0, 0)
            top_part = jnp.where(col_index == (first + 1) % col_count, panel_cols[:block], 0.0)
            stacked = jnp.concatenate([gram_part, top_part]).reshape(col_count, small, block)
            total = exchange(stacked, "col").sum(0)
            copies = jnp.broadcast_to(total[None], (col_count, small, block))
            gram_and_top = exchange(copies, "col").reshape(2 * block, block)
            panel_rows = next_rows - dot(jnp.concatenate([reflect_rows, companion_rows], axis=1), tile_factor, 1, 1)
        left_factor = jnp.concatenate([reflect_rows, companion_rows], axis=1)
        right_factor = jnp.concatenate([companion_cols, reflect_cols], axis=1)
        current = current - dot(left_factor, right_factor, 1, 1)
    return current.reshape(matrix.shape)


def solution(mesh):
    in_specs = (P(None, "row", None, None, "col", None),)
    out_specs = P(None, "row", None, None, "col", None)
    return jax.shard_map(local, mesh=mesh, in_specs=in_specs, out_specs=out_specs, check_vma=False)
```

```python
import functools

import jax
import jax.numpy as jnp
from jax import lax
from jax.experimental import pallas as pl
from jax.experimental.pallas import tpu as pltpu
from jax.sharding import PartitionSpec as P

newton_sweeps = 8
pivot_group = 4


def dot(left_side, right_side, left_dim=1, right_dim=0):
    return lax.dot_general(
        left_side,
        right_side,
        (((left_dim,), (right_dim,)), ((), ())),
        precision=lax.Precision.HIGHEST,
        preferred_element_type=jnp.float32,
    )


def halves_of(values):
    high = values.astype(jnp.bfloat16)
    return high, (values - high.astype(jnp.float32)).astype(jnp.bfloat16)


def wide_dot(left_side, right_side, right_dim=0):
    left_high, left_low = halves_of(left_side)
    right_high, right_low = halves_of(right_side)

    def product(first, second):
        return lax.dot_general(
            first, second, (((1,), (right_dim,)), ((), ())), preferred_element_type=jnp.float32
        )

    return product(left_high, right_high) + (product(left_high, right_low) + product(left_low, right_high))


def newton_inverse(middle):
    identity = jnp.eye(middle.shape[0], dtype=jnp.float32)
    power = identity - middle
    approx = identity + power
    for sweep_step in range(1, newton_sweeps):
        power = dot(power, power)
        approx = approx + dot(approx, power)
    return approx


def exchange(chunks, axis):
    return lax.all_to_all(chunks, axis, 0, 0)


def eye_of(block):
    row = lax.broadcasted_iota(jnp.int32, (block, block), 0)
    lane = lax.broadcasted_iota(jnp.int32, (block, block), 1)
    return jnp.where(row == lane, 1.0, 0.0).astype(jnp.float32)


def factor_inverse(gram, scratch):
    block = gram.shape[0]
    tiles = block // 8
    shape = (8, block)
    lane = lax.broadcasted_iota(jnp.int32, shape, 1)
    sub = lax.broadcasted_iota(jnp.int32, shape, 0)
    left = [gram[8 * b : 8 * b + 8] for b in range(tiles)]
    right = [jnp.where(lane == sub + 8 * b, 1.0, 0.0).astype(jnp.float32) for b in range(tiles)]
    members = range(pivot_group)
    for start in range(0, block, pivot_group):
        home, top = start // 8, start % 8
        pivots = [jnp.broadcast_to(left[home][top + i : top + i + 1], shape) for i in members]
        shadows = [jnp.broadcast_to(right[home][top + i : top + i + 1], shape) for i in members]
        corner = [
            [
                jnp.broadcast_to(left[home][top + i : top + i + 1, start + m : start + m + 1], shape)
                for m in members
            ]
            for i in members
        ]
        inverse = []
        for i in members:
            root = lax.rsqrt(corner[i][i])
            inverse.append(root * root)
            scratch[start + i : start + i + 1, :] = (shadows[i] * root)[0:1]
            for j in range(i + 1, pivot_group):
                factor = corner[j][i] * inverse[i]
                pivots[j] = pivots[j] - factor * pivots[i]
                shadows[j] = shadows[j] - factor * shadows[i]
                for m in range(i + 1, pivot_group):
                    corner[j][m] = corner[j][m] - factor * corner[i][m]
        for b in range((start + pivot_group) // 8, tiles):
            column = [jnp.broadcast_to(left[b][:, start + i : start + i + 1], shape) for i in members]
            for i in members:
                factor = column[i] * inverse[i]
                for m in range(i + 1, pivot_group):
                    column[m] = column[m] - factor * corner[i][m]
                left[b] = left[b] - factor * pivots[i]
                right[b] = right[b] - factor * shadows[i]
    return scratch[...]


def launch(body, shapes, place, *operands, scratch=None):
    outs = [jax.ShapeDtypeStruct(shape, jnp.float32) for shape in shapes]

    def kernel(*refs):
        extra = refs[len(refs) - 1 :] if scratch else ()
        inputs = refs[1 : 1 + len(operands)]
        results = body(refs[0], *[ref[...] for ref in inputs], *extra)
        for ref, value in zip(refs[1 + len(operands) : 1 + len(operands) + len(outs)], results, strict=True):
            ref[...] = value

    vmem = pl.BlockSpec(memory_space=pltpu.VMEM)
    return pl.pallas_call(
        kernel,
        out_shape=outs,
        in_specs=[pl.BlockSpec(memory_space=pltpu.SMEM)] + [vmem] * len(operands),
        out_specs=[vmem] * len(outs),
        scratch_shapes=[pltpu.VMEM(scratch, jnp.float32)] if scratch else [],
    )(place, *operands)


def first_tile(values, block, change):
    return jnp.concatenate([change(values[:block]), values[block:]])


def keep_from(values, block, index, first):
    return first_tile(values, block, lambda tile: tile * jnp.where(index >= first, 1.0, 0.0))


def front_body(place, stacked, panel_even, panel_odd, panel_cols, current, scratch, *, first, last, sizes):
    block, spread, part, col_count, small, tile_cols = sizes
    identity = eye_of(block)
    lower_inverse = factor_inverse(stacked[:block], scratch)
    pivot_tile = identity + dot(stacked[block:], lower_inverse, 1, 1)

    def reflect(panel, index):
        q = dot(keep_from(panel, block, index, first), lower_inverse, 1, 1)
        return first_tile(q, block, lambda tile: tile + identity * jnp.where(index == first, 1.0, 0.0))

    cols = reflect(panel_cols, place[1])
    even = reflect(panel_even, place[0])
    odd = dot(panel_odd, lower_inverse, 1, 1)
    product = wide_dot(current, cols)
    tiles = [product[block * t : block * t + block] for t in range(spread * tile_cols)]
    sums = [jnp.concatenate(tiles[h::spread]) for h in range(spread)]
    cross = dot(even.T, sums[0]) + dot(odd.T, sums[1])
    if last:
        pivot_rows = jnp.zeros_like(cross)
    else:
        pivot_rows = tiles[0] * jnp.where(place[0] == first, 1.0, 0.0)
    little = jnp.concatenate([cross, pivot_rows]).reshape(col_count, small, block)
    send = jnp.concatenate([each.reshape(col_count, part, block) for each in sums] + [little], axis=1)
    return send, even, odd, cols, pivot_tile


def split_shared(got, start, sizes):
    block, spread, part, col_count, small, tile_cols = sizes
    pieces = [
        got[:, start + part * h : start + part * h + part].reshape(col_count * part, block) for h in range(spread + 1)
    ]
    return pieces[:spread], pieces[spread]


def companions(got, inverse_core, even, odd, cols, core_block, sizes):
    (w_even, w_odd), w_cols = split_shared(got, 0, sizes)
    pairs = ((w_even, even), (w_odd, odd), (w_cols, cols))
    return [dot(w, inverse_core, 1, 1) - 0.5 * dot(v, core_block) for w, v in pairs]


def middle_body(place, got, inverse_core, cols, pivot_tile, shared, *, first, sizes):
    block, spread, part, col_count, small, tile_cols = sizes
    little = got[:, (spread + 1) * part :].reshape(col_count * small, block)
    core_block = dot(dot(inverse_core, little[:block]), inverse_core, 1, 1)
    w_cols = split_shared(got, 0, sizes)[1]
    companion = dot(w_cols, inverse_core, 1, 1) - 0.5 * dot(cols, core_block)
    companion_tile = dot(little[block:], inverse_core, 1, 1) - 0.5 * dot(pivot_tile, core_block)
    panel = split_shared(shared, (spread + 1) * part, sizes)[1]
    panel = panel - (dot(cols, companion_tile, 1, 1) + dot(companion, pivot_tile, 1, 1))
    masked = keep_from(panel, block, place[1], first + 1)
    gram = dot(masked.T, masked)
    top = panel[:block] * jnp.where(place[1] == first + 1, 1.0, 0.0)
    send = jnp.concatenate([gram, top]).reshape(col_count, small, block)
    return send, core_block, companion_tile, panel


def update_tiles(current, even, odd, even_z, odd_z, cols, cols_z, sizes):
    block, spread, part, col_count, small, tile_cols = sizes
    right = jnp.concatenate([cols_z, cols], axis=1)
    lefts = [jnp.concatenate([even, even_z], axis=1), jnp.concatenate([odd, odd_z], axis=1)]
    pieces = [lefts[h][block * u : block * u + block] for u in range(tile_cols) for h in range(spread)]
    return current - wide_dot(jnp.concatenate(pieces), right, 1)


def between_body(place, current, got, inverse_core, core_block, even, odd, cols, companion_tile, pivot_tile, shared, *, sizes):
    block, spread, part, col_count, small, tile_cols = sizes
    even_z, odd_z, cols_z = companions(got, inverse_core, even, odd, cols, core_block, sizes)
    (next_even, next_odd), unused = split_shared(shared, (spread + 1) * part, sizes)
    panels = [
        values - (dot(v, companion_tile, 1, 1) + dot(z, pivot_tile, 1, 1))
        for values, v, z in ((next_even, even, even_z), (next_odd, odd, odd_z))
    ]
    return update_tiles(current, even, odd, even_z, odd_z, cols, cols_z, sizes), panels[0], panels[1]


def final_body(place, current, got, inverse_core, even, odd, cols, *, sizes):
    block, spread, part, col_count, small, tile_cols = sizes
    cross = got[:, (spread + 1) * part :].reshape(col_count * small, block)[:block]
    core_block = dot(dot(inverse_core, cross), inverse_core, 1, 1)
    even_z, odd_z, cols_z = companions(got, inverse_core, even, odd, cols, core_block, sizes)
    return (update_tiles(current, even, odd, even_z, odd_z, cols, cols_z, sizes),)


def local(matrix):
    tile_rows, block, tile_cols = matrix.shape[0], matrix.shape[2], matrix.shape[3]
    rows, cols = tile_rows * block, tile_cols * block
    row_count, col_count = lax.axis_size("row"), lax.axis_size("col")
    row_index, col_index = lax.axis_index("row"), lax.axis_index("col")
    spread = col_count // row_count
    part = cols // col_count
    chunk = spread * part
    small = 2 * block // col_count
    sizes = (block, spread, part, col_count, small, tile_cols)
    place = jnp.stack([row_index, col_index]).astype(jnp.int32)
    tall = (cols, block)
    tile = (block, block)

    def chunks_of(values):
        split = values.reshape(tile_cols, spread, block // part, part, block)
        return split.transpose(0, 2, 1, 3, 4).reshape(col_count, chunk, block)

    def share(mine, count):
        got = exchange(jnp.broadcast_to(mine[None], (row_count,) + mine.shape), "row")
        sends = []
        for index in range(count):
            piece = mine[index * chunk : (index + 1) * chunk]
            sends.append(jnp.broadcast_to(piece[None], (col_count, chunk, block)))
            wanted = got[:, index * chunk : (index + 1) * chunk].reshape(row_count, spread, part, block)
            sends.append(wanted.transpose(1, 0, 2, 3).reshape(col_count, part, block))
        total = got[:, count * chunk :].sum(0)
        sends.append(jnp.broadcast_to(total[None], (col_count,) + total.shape))
        return exchange(jnp.concatenate(sends, axis=1), "col")

    current = matrix.reshape(rows, cols)

    own_col = current[:, :block]
    tile_ids = jnp.repeat(jnp.arange(tile_rows, dtype=jnp.int32) * row_count + row_index, block)[:, None]
    masked = jnp.where(tile_ids >= 1, own_col, 0.0)
    gram_part = dot(masked, masked, 0, 0)
    top_part = jnp.where(row_index == 1, own_col[:block], 0.0)
    stacked = jnp.concatenate([gram_part, top_part]).reshape(col_count, small, block)
    got = exchange(jnp.concatenate([chunks_of(own_col), stacked], axis=1), "col")
    shared = share(jnp.concatenate([got[0, :chunk], got[1, :chunk], got[0, chunk:]]), 2)
    stacked = shared[:, 2 * (chunk + part) :].reshape(2 * block, block)
    even, odd = (shared[:, part * h : part * h + part].reshape(cols, block) for h in range(spread))
    panel_cols = shared[:, chunk : chunk + part].reshape(cols, block)

    for panel_index in range(2):
        last = panel_index == 1
        first = panel_index + 1
        send, even, odd, panel_cols, pivot_tile = launch(
            functools.partial(front_body, first=first, last=last, sizes=sizes),
            [(col_count, chunk + small, block), tall, tall, tall, tile],
            place, stacked, even, odd, panel_cols, current, scratch=tile,
        )
        inverse_core = newton_inverse(pivot_tile)
        got = share(exchange(send, "col").sum(0), 1)
        if last:
            (current,) = launch(
                functools.partial(final_body, sizes=sizes),
                [(rows, cols)],
                place, current, got, inverse_core, even, odd, panel_cols,
            )
            break
        send, core_block, companion_tile, next_cols = launch(
            functools.partial(middle_body, first=first, sizes=sizes),
            [(col_count, small, block), tile, tile, tall],
            place, got, inverse_core, panel_cols, pivot_tile, shared,
        )
        total = exchange(send, "col").sum(0)
        copies = jnp.broadcast_to(total[None], (col_count, small, block))
        stacked = exchange(copies, "col").reshape(2 * block, block)
        current, even, odd = launch(
            functools.partial(between_body, sizes=sizes),
            [(rows, cols), tall, tall],
            place, current, got, inverse_core, core_block, even, odd, panel_cols, companion_tile, pivot_tile, shared,
        )
        panel_cols = next_cols
    return current.reshape(matrix.shape)


def solution(mesh):
    in_specs = (P(None, "row", None, None, "col", None),)
    out_specs = P(None, "row", None, None, "col", None)
    return jax.shard_map(local, mesh=mesh, in_specs=in_specs, out_specs=out_specs, check_vma=False)
```

```python
import functools

import jax
import jax.numpy as jnp
from jax import lax
from jax.experimental import pallas as pl
from jax.experimental.pallas import tpu as pltpu
from jax.sharding import PartitionSpec as P

newton_sweeps = 8
pivot_group = 4


def dot(left_side, right_side, left_dim=1, right_dim=0):
    return lax.dot_general(
        left_side,
        right_side,
        (((left_dim,), (right_dim,)), ((), ())),
        precision=lax.Precision.HIGHEST,
        preferred_element_type=jnp.float32,
    )


def halves_of(values):
    high = values.astype(jnp.bfloat16)
    return high, (values - high.astype(jnp.float32)).astype(jnp.bfloat16)


def wide_dot(left_side, right_side, right_dim=0):
    left_high, left_low = halves_of(left_side)
    right_high, right_low = halves_of(right_side)

    def product(first, second):
        return lax.dot_general(
            first, second, (((1,), (right_dim,)), ((), ())), preferred_element_type=jnp.float32
        )

    return product(left_high, right_high) + (product(left_high, right_low) + product(left_low, right_high))


def newton_body(place, middle):
    identity = eye_of(middle.shape[0])
    power = identity - middle

    approx = identity + power
    for sweep_step in range(1, newton_sweeps):
        power = dot(power, power)
        approx = approx + dot(approx, power)
    return (approx,)


def exchange(chunks, axis):
    return lax.all_to_all(chunks, axis, 0, 0)


def eye_of(block):
    row = lax.broadcasted_iota(jnp.int32, (block, block), 0)
    lane = lax.broadcasted_iota(jnp.int32, (block, block), 1)
    return jnp.where(row == lane, 1.0, 0.0).astype(jnp.float32)


def factor_inverse(gram, scratch):
    block = gram.shape[0]
    tiles = block // 8
    shape = (8, block)
    lane = lax.broadcasted_iota(jnp.int32, shape, 1)
    sub = lax.broadcasted_iota(jnp.int32, shape, 0)
    left = [gram[8 * b : 8 * b + 8] for b in range(tiles)]
    right = [jnp.where(lane == sub + 8 * b, 1.0, 0.0).astype(jnp.float32) for b in range(tiles)]
    members = range(pivot_group)
    for start in range(0, block, pivot_group):
        home, top = start // 8, start % 8
        pivots = [jnp.broadcast_to(left[home][top + i : top + i + 1], shape) for i in members]
        shadows = [jnp.broadcast_to(right[home][top + i : top + i + 1], shape) for i in members]
        corner = [
            [
                jnp.broadcast_to(left[home][top + i : top + i + 1, start + m : start + m + 1], shape)
                for m in members
            ]
            for i in members
        ]
        inverse = []
        for i in members:
            root = lax.rsqrt(corner[i][i])
            inverse.append(root * root)
            scratch[start + i : start + i + 1, :] = (shadows[i] * root)[0:1]
            for j in range(i + 1, pivot_group):
                factor = corner[j][i] * inverse[i]
                pivots[j] = pivots[j] - factor * pivots[i]
                shadows[j] = shadows[j] - factor * shadows[i]
                for m in range(i + 1, pivot_group):
                    corner[j][m] = corner[j][m] - factor * corner[i][m]
        for b in range((start + pivot_group) // 8, tiles):
            column = [jnp.broadcast_to(left[b][:, start + i : start + i + 1], shape) for i in members]
            for i in members:
                factor = column[i] * inverse[i]
                for m in range(i + 1, pivot_group):
                    column[m] = column[m] - factor * corner[i][m]
                left[b] = left[b] - factor * pivots[i]
                right[b] = right[b] - factor * shadows[i]
    return scratch[...]


def launch(body, shapes, place, *operands, scratch=None, lines=None):
    outs = [jax.ShapeDtypeStruct(shape, jnp.float32) for shape in shapes]

    def kernel(*refs):
        extra = refs[len(refs) - 1 :] if scratch else ()
        inputs = refs[1 : 1 + len(operands)]
        results = body(refs[0], *[ref[...] for ref in inputs], *extra)
        for ref, value in zip(refs[1 + len(operands) : 1 + len(operands) + len(outs)], results, strict=True):
            if lines:
                width = value.shape[1] // lines
                for u in range(lines):
                    ref[pl.ds(u, value.shape[0], stride=lines), :] = value[:, u * width : (u + 1) * width]
            else:
                ref[...] = value

    vmem = pl.BlockSpec(memory_space=pltpu.VMEM)
    return pl.pallas_call(
        kernel,
        out_shape=outs,
        in_specs=[pl.BlockSpec(memory_space=pltpu.SMEM)] + [vmem] * len(operands),
        out_specs=[vmem] * len(outs),
        scratch_shapes=[pltpu.VMEM(scratch, jnp.float32)] if scratch else [],
    )(place, *operands)


def first_tile(values, block, change):
    return jnp.concatenate([change(values[:block]), values[block:]])


def keep_from(values, block, index, first):
    return first_tile(values, block, lambda tile: tile * jnp.where(index >= first, 1.0, 0.0))


def front_body(place, stacked, panel_even, panel_odd, panel_cols, current, scratch, *, first, last, sizes):
    block, spread, part, col_count, small, tile_cols = sizes
    identity = eye_of(block)
    lower_inverse = factor_inverse(stacked[:block], scratch)
    pivot_tile = identity + dot(stacked[block:], lower_inverse, 1, 1)

    def reflect(panel, index):
        q = dot(keep_from(panel, block, index, first), lower_inverse, 1, 1)
        return first_tile(q, block, lambda tile: tile + identity * jnp.where(index == first, 1.0, 0.0))

    if panel_cols.shape[0] == block:
        panel_cols = panel_cols.T
    cols = reflect(panel_cols, place[1])
    even = reflect(panel_even, place[0])
    odd = dot(panel_odd, lower_inverse, 1, 1)
    product = wide_dot(current, cols)
    tiles = [product[block * t : block * t + block] for t in range(spread * tile_cols)]
    sums = [jnp.concatenate(tiles[h::spread]) for h in range(spread)]
    cross = dot(even.T, sums[0]) + dot(odd.T, sums[1])
    if last:
        pivot_rows = jnp.zeros_like(cross)
    else:
        pivot_rows = tiles[0] * jnp.where(place[0] == first, 1.0, 0.0)
    little = jnp.concatenate([cross, pivot_rows]).reshape(col_count, small, block)
    send = jnp.concatenate([each.reshape(col_count, part, block) for each in sums] + [little], axis=1)
    return send, even, odd, cols, pivot_tile


def split_shared(got, start, sizes):
    block, spread, part, col_count, small, tile_cols = sizes
    pieces = [
        got[:, start + part * h : start + part * h + part].reshape(col_count * part, block) for h in range(spread + 1)
    ]
    return pieces[:spread], pieces[spread]


def companions(got, inverse_core, even, odd, cols, core_block, sizes):
    (w_even, w_odd), w_cols = split_shared(got, 0, sizes)
    pairs = ((w_even, even), (w_odd, odd), (w_cols, cols))
    return [dot(w, inverse_core, 1, 1) - 0.5 * dot(v, core_block) for w, v in pairs]


def middle_body(place, got, inverse_core, cols, pivot_tile, next_tile, *, first, sizes):
    block, spread, part, col_count, small, tile_cols = sizes
    little = got[:, (spread + 1) * part :].reshape(col_count * small, block)
    core_block = dot(dot(inverse_core, little[:block]), inverse_core, 1, 1)
    w_cols = split_shared(got, 0, sizes)[1]
    companion = dot(w_cols, inverse_core, 1, 1) - 0.5 * dot(cols, core_block)
    companion_tile = dot(little[block:], inverse_core, 1, 1) - 0.5 * dot(pivot_tile, core_block)
    panel = next_tile.T - (dot(cols, companion_tile, 1, 1) + dot(companion, pivot_tile, 1, 1))
    masked = keep_from(panel, block, place[1], first + 1)
    gram = dot(masked.T, masked)
    top = panel[:block] * jnp.where(place[1] == first + 1, 1.0, 0.0)
    send = jnp.concatenate([gram, top]).reshape(col_count, small, block)
    return send, core_block, companion_tile, panel


def update_tiles(current, even, odd, even_z, odd_z, cols, cols_z, sizes):
    block, spread, part, col_count, small, tile_cols = sizes
    right = jnp.concatenate([cols_z, cols], axis=1)
    lefts = [jnp.concatenate([even, even_z], axis=1), jnp.concatenate([odd, odd_z], axis=1)]
    pieces = [lefts[h][block * u : block * u + block] for u in range(tile_cols) for h in range(spread)]
    return current - wide_dot(jnp.concatenate(pieces), right, 1)


def between_body(place, current, got, inverse_core, core_block, even, odd, cols, companion_tile, pivot_tile, shared, *, sizes):
    block, spread, part, col_count, small, tile_cols = sizes
    even_z, odd_z, cols_z = companions(got, inverse_core, even, odd, cols, core_block, sizes)
    next_even, next_odd = (
        shared[:, part * h : part * h + part].reshape(col_count * part, block) for h in range(spread)
    )
    panels = [
        values - (dot(v, companion_tile, 1, 1) + dot(z, pivot_tile, 1, 1))
        for values, v, z in ((next_even, even, even_z), (next_odd, odd, odd_z))
    ]
    return update_tiles(current, even, odd, even_z, odd_z, cols, cols_z, sizes), panels[0], panels[1]


def final_body(place, current, got, inverse_core, even, odd, cols, *, sizes):
    block, spread, part, col_count, small, tile_cols = sizes
    cross = got[:, (spread + 1) * part :].reshape(col_count * small, block)[:block]
    core_block = dot(dot(inverse_core, cross), inverse_core, 1, 1)
    even_z, odd_z, cols_z = companions(got, inverse_core, even, odd, cols, core_block, sizes)
    return (update_tiles(current, even, odd, even_z, odd_z, cols, cols_z, sizes),)


def local(matrix):
    tile_rows, block, tile_cols = matrix.shape[0], matrix.shape[2], matrix.shape[3]
    rows, cols = tile_rows * block, tile_cols * block
    row_count, col_count = lax.axis_size("row"), lax.axis_size("col")
    row_index, col_index = lax.axis_index("row"), lax.axis_index("col")
    spread = col_count // row_count
    part = cols // col_count
    chunk = spread * part
    small = 2 * block // col_count
    sizes = (block, spread, part, col_count, small, tile_cols)
    place = jnp.stack([row_index, col_index]).astype(jnp.int32)
    tall = (cols, block)
    tile = (block, block)

    def chunks_of(values):
        split = values.reshape(tile_cols, spread, block // part, part, block)
        return split.transpose(0, 2, 1, 3, 4).reshape(col_count, chunk, block)

    def copies_of(value, count):
        return jnp.broadcast_to(value[None], (count,) + value.shape)

    def share(mine, got):
        wanted = got[:, :chunk].reshape(row_count, spread, part, block)
        wanted = wanted.transpose(1, 0, 2, 3).reshape(col_count, part, block)
        total = got[:, chunk:].sum(0)
        sends = [copies_of(mine[:chunk], col_count), wanted, copies_of(total, col_count)]
        return exchange(jnp.concatenate(sends, axis=1), "col")

    def only_at(value, source):
        return jnp.where(row_index == source, value, 0.0)

    def hop(held, source, step):
        if step >= row_count:
            return held
        pairs = [((source + k) % row_count, (source + k + step) % row_count) for k in range(0, row_count, 2 * step)]
        return held + lax.ppermute(held, "row", pairs)

    def after(value, held):
        return lax.optimization_barrier((value, held))

    current = matrix.reshape(rows, cols)

    own_col = current[:, :block]
    tile_ids = jnp.repeat(jnp.arange(tile_rows, dtype=jnp.int32) * row_count + row_index, block)[:, None]
    masked = jnp.where(tile_ids >= 1, own_col, 0.0)
    gram_part = dot(masked, masked, 0, 0)
    top_part = jnp.where(row_index == 1, own_col[:block], 0.0)
    stacked = jnp.concatenate([gram_part, top_part]).reshape(col_count, small, block)
    got = exchange(jnp.concatenate([chunks_of(own_col), stacked], axis=1), "col")
    got, panel_cols = after(got, hop(only_at(current[:block], 0), 0, 8))
    next_chunk = got[1, :chunk]
    total = exchange(copies_of(got[0, chunk:], row_count), "row")
    total, panel_cols = after(total, hop(panel_cols, 0, 4))
    total = total.sum(0)
    shared = exchange(copies_of(jnp.concatenate([got[0, :chunk], total]), col_count), "col")
    panel_cols = hop(hop(panel_cols, 0, 2), 0, 1)
    shared, next_tile = after(shared, only_at(current[:block], 1))
    stacked = shared[:, chunk:].reshape(2 * block, block)
    even, odd = (shared[:, part * h : part * h + part].reshape(cols, block) for h in range(spread))

    for panel_index in range(2):
        last = panel_index == 1
        first = panel_index + 1
        send, even, odd, panel_cols, pivot_tile = launch(
            functools.partial(front_body, first=first, last=last, sizes=sizes),
            [(col_count, chunk + small, block), tall, tall, tall, tile],
            place, stacked, even, odd, panel_cols, current, scratch=tile,
        )
        (inverse_core,) = launch(newton_body, [tile], place, pivot_tile)
        if last:
            mine = exchange(send, "col").sum(0)
            got = share(mine, exchange(copies_of(mine, row_count), "row"))
        else:
            send, next_tile = after(send, hop(next_tile, 1, 8))
            mine, next_tile = after(exchange(send, "col"), hop(next_tile, 1, 4))
            mine = mine.sum(0)
            rest, next_tile = after(exchange(copies_of(mine, row_count), "row"), hop(next_tile, 1, 2))
            got, next_tile = after(share(mine, rest), hop(next_tile, 1, 1))
        if last:
            (current,) = launch(
                functools.partial(final_body, sizes=sizes),
                [(rows * tile_cols, block)],
                place, current, got, inverse_core, even, odd, panel_cols, lines=tile_cols,
            )
            break
        send, core_block, companion_tile, next_cols = launch(
            functools.partial(middle_body, first=first, sizes=sizes),
            [(col_count, small, block), tile, tile, tall],
            place, got, inverse_core, panel_cols, pivot_tile, next_tile,
        )
        shared = exchange(jnp.concatenate([copies_of(next_chunk, col_count), send], axis=1), "col")
        total = shared[:, chunk:].sum(0)
        stacked = exchange(copies_of(total, col_count), "col").reshape(2 * block, block)
        current, even, odd = launch(
            functools.partial(between_body, sizes=sizes),
            [(rows, cols), tall, tall],
            place, current, got, inverse_core, core_block, even, odd, panel_cols, companion_tile, pivot_tile, shared,
        )
        panel_cols = next_cols
    return current.reshape(matrix.shape)


def solution(mesh):
    in_specs = (P(None, "row", None, None, "col", None),)
    out_specs = P(None, "row", None, None, "col", None)
    return jax.shard_map(local, mesh=mesh, in_specs=in_specs, out_specs=out_specs, check_vma=False)
```

```python
import functools

import jax
import jax.numpy as jnp
from jax import lax
from jax.experimental import pallas as pl
from jax.experimental.pallas import tpu as pltpu
from jax.sharding import PartitionSpec as P

newton_sweeps = 8
pivot_group = 4


def dot(left_side, right_side, left_dim=1, right_dim=0):
    return lax.dot_general(
        left_side,
        right_side,
        (((left_dim,), (right_dim,)), ((), ())),
        precision=lax.Precision.HIGHEST,
        preferred_element_type=jnp.float32,
    )


def halves_of(values):
    high = values.astype(jnp.bfloat16)
    return high, (values - high.astype(jnp.float32)).astype(jnp.bfloat16)


def wide_dot(left_side, right_side, right_dim=0):
    left_high, left_low = halves_of(left_side)
    right_high, right_low = halves_of(right_side)

    def product(first, second):
        return lax.dot_general(
            first, second, (((1,), (right_dim,)), ((), ())), preferred_element_type=jnp.float32
        )

    return product(left_high, right_high) + (product(left_high, right_low) + product(left_low, right_high))


def newton_body(place, middle):
    identity = eye_of(middle.shape[0])
    power = identity - middle

    approx = identity + power
    for sweep_step in range(1, newton_sweeps):
        power = dot(power, power)
        approx = approx + dot(approx, power)
    return (approx,)


def exchange(chunks, axis):
    return lax.all_to_all(chunks, axis, 0, 0)


def eye_of(block):
    row = lax.broadcasted_iota(jnp.int32, (block, block), 0)
    lane = lax.broadcasted_iota(jnp.int32, (block, block), 1)
    return jnp.where(row == lane, 1.0, 0.0).astype(jnp.float32)


def factor_inverse(gram, scratch):
    block = gram.shape[0]
    tiles = block // 8
    shape = (8, block)
    lane = lax.broadcasted_iota(jnp.int32, shape, 1)
    sub = lax.broadcasted_iota(jnp.int32, shape, 0)
    left = [gram[8 * b : 8 * b + 8] for b in range(tiles)]
    right = [jnp.where(lane == sub + 8 * b, 1.0, 0.0).astype(jnp.float32) for b in range(tiles)]
    members = range(pivot_group)
    for start in range(0, block, pivot_group):
        home, top = start // 8, start % 8
        pivots = [jnp.broadcast_to(left[home][top + i : top + i + 1], shape) for i in members]
        shadows = [jnp.broadcast_to(right[home][top + i : top + i + 1], shape) for i in members]
        corner = [
            [
                jnp.broadcast_to(left[home][top + i : top + i + 1, start + m : start + m + 1], shape)
                for m in members
            ]
            for i in members
        ]
        inverse = []
        for i in members:
            root = lax.rsqrt(corner[i][i])
            inverse.append(root * root)
            scratch[start + i : start + i + 1, :] = (shadows[i] * root)[0:1]
            for j in range(i + 1, pivot_group):
                factor = corner[j][i] * inverse[i]
                pivots[j] = pivots[j] - factor * pivots[i]
                shadows[j] = shadows[j] - factor * shadows[i]
                for m in range(i + 1, pivot_group):
                    corner[j][m] = corner[j][m] - factor * corner[i][m]
        for b in range((start + pivot_group) // 8, tiles):
            column = [jnp.broadcast_to(left[b][:, start + i : start + i + 1], shape) for i in members]
            for i in members:
                factor = column[i] * inverse[i]
                for m in range(i + 1, pivot_group):
                    column[m] = column[m] - factor * corner[i][m]
                left[b] = left[b] - factor * pivots[i]
                right[b] = right[b] - factor * shadows[i]
    return scratch[...]


def launch(body, shapes, place, *operands, scratch=None, lines=None):
    outs = [jax.ShapeDtypeStruct(shape, jnp.float32) for shape in shapes]

    def kernel(*refs):
        extra = refs[len(refs) - 1 :] if scratch else ()
        inputs = refs[1 : 1 + len(operands)]
        results = body(refs[0], *[ref[...] for ref in inputs], *extra)
        for ref, value in zip(refs[1 + len(operands) : 1 + len(operands) + len(outs)], results, strict=True):
            if lines:
                width = value.shape[1] // lines
                for u in range(lines):
                    ref[pl.ds(u, value.shape[0], stride=lines), :] = value[:, u * width : (u + 1) * width]
            else:
                ref[...] = value

    vmem = pl.BlockSpec(memory_space=pltpu.VMEM)
    return pl.pallas_call(
        kernel,
        out_shape=outs,
        in_specs=[pl.BlockSpec(memory_space=pltpu.SMEM)] + [vmem] * len(operands),
        out_specs=[vmem] * len(outs),
        scratch_shapes=[pltpu.VMEM(scratch, jnp.float32)] if scratch else [],
    )(place, *operands)


def first_tile(values, block, change):
    return jnp.concatenate([change(values[:block]), values[block:]])


def keep_from(values, block, index, first):
    return first_tile(values, block, lambda tile: tile * jnp.where(index >= first, 1.0, 0.0))


def front_body(place, stacked, panel_even, panel_odd, panel_cols, current, scratch, *, first, last, sizes):
    block, spread, part, col_count, small, tile_cols = sizes
    identity = eye_of(block)
    lower_inverse = factor_inverse(stacked[:block], scratch)
    pivot_tile = identity + dot(stacked[block:], lower_inverse, 1, 1)

    def reflect(panel, index):
        q = dot(keep_from(panel, block, index, first), lower_inverse, 1, 1)
        return first_tile(q, block, lambda tile: tile + identity * jnp.where(index == first, 1.0, 0.0))

    cols = reflect(panel_cols, place[1])
    even = reflect(panel_even, place[0])
    odd = dot(panel_odd, lower_inverse, 1, 1)
    product = wide_dot(current, cols)
    tiles = [product[block * t : block * t + block] for t in range(spread * tile_cols)]
    sums = [jnp.concatenate(tiles[h::spread]) for h in range(spread)]
    cross = wide_dot(even.T, sums[0]) + wide_dot(odd.T, sums[1])
    if last:
        pivot_rows = jnp.zeros_like(cross)
    else:
        pivot_rows = tiles[0] * jnp.where(place[0] == first, 1.0, 0.0)
    little = jnp.concatenate([cross, pivot_rows]).reshape(col_count, small, block)
    send = jnp.concatenate([each.reshape(col_count, part, block) for each in sums] + [little], axis=1)
    return send, even, odd, cols, pivot_tile


def split_shared(got, start, sizes):
    block, spread, part, col_count, small, tile_cols = sizes
    pieces = [
        got[:, start + part * h : start + part * h + part].reshape(col_count * part, block) for h in range(spread + 1)
    ]
    return pieces[:spread], pieces[spread]


def companions(got, inverse_core, even, odd, cols, core_block, sizes):
    (w_even, w_odd), w_cols = split_shared(got, 0, sizes)
    pairs = ((w_even, even), (w_odd, odd), (w_cols, cols))
    return [dot(w, inverse_core, 1, 1) - 0.5 * dot(v, core_block) for w, v in pairs]


def middle_body(place, got, inverse_core, cols, pivot_tile, *, first, sizes):
    block, spread, part, col_count, small, tile_cols = sizes
    after = (spread + 1) * part
    little = got[:, after : after + small].reshape(col_count * small, block)
    core_block = dot(dot(inverse_core, little[:block]), inverse_core, 1, 1)
    w_cols = split_shared(got, 0, sizes)[1]
    companion = dot(w_cols, inverse_core, 1, 1) - 0.5 * dot(cols, core_block)
    companion_tile = dot(little[block:], inverse_core, 1, 1) - 0.5 * dot(pivot_tile, core_block)
    panel = got[:, after + small :].reshape(col_count * part, block) - (dot(cols, companion_tile, 1, 1) + dot(companion, pivot_tile, 1, 1))
    masked = keep_from(panel, block, place[1], first + 1)
    gram = dot(masked.T, masked)
    top = panel[:block] * jnp.where(place[1] == first + 1, 1.0, 0.0)
    send = jnp.concatenate([gram, top]).reshape(col_count, small, block)
    return send, core_block, companion_tile, panel


def update_tiles(current, even, odd, even_z, odd_z, cols, cols_z, sizes):
    block, spread, part, col_count, small, tile_cols = sizes
    right = jnp.concatenate([cols_z, cols], axis=1)
    lefts = [jnp.concatenate([even, even_z], axis=1), jnp.concatenate([odd, odd_z], axis=1)]
    pieces = [lefts[h][block * u : block * u + block] for u in range(tile_cols) for h in range(spread)]
    return current - wide_dot(jnp.concatenate(pieces), right, 1)


def between_body(place, current, got, inverse_core, core_block, even, odd, cols, companion_tile, pivot_tile, shared, *, sizes):
    block, spread, part, col_count, small, tile_cols = sizes
    even_z, odd_z, cols_z = companions(got, inverse_core, even, odd, cols, core_block, sizes)
    next_even, next_odd = (
        shared[:, part * h : part * h + part].reshape(col_count * part, block) for h in range(spread)
    )
    panels = [
        values - (dot(v, companion_tile, 1, 1) + dot(z, pivot_tile, 1, 1))
        for values, v, z in ((next_even, even, even_z), (next_odd, odd, odd_z))
    ]
    return update_tiles(current, even, odd, even_z, odd_z, cols, cols_z, sizes), panels[0], panels[1]


def final_body(place, current, got, inverse_core, even, odd, cols, *, sizes):
    block, spread, part, col_count, small, tile_cols = sizes
    cross = got[:, (spread + 1) * part :].reshape(col_count * small, block)[:block]
    core_block = dot(dot(inverse_core, cross), inverse_core, 1, 1)
    even_z, odd_z, cols_z = companions(got, inverse_core, even, odd, cols, core_block, sizes)
    return (update_tiles(current, even, odd, even_z, odd_z, cols, cols_z, sizes),)


def local(matrix):
    tile_rows, block, tile_cols = matrix.shape[0], matrix.shape[2], matrix.shape[3]
    rows, cols = tile_rows * block, tile_cols * block
    row_count, col_count = lax.axis_size("row"), lax.axis_size("col")
    row_index, col_index = lax.axis_index("row"), lax.axis_index("col")
    spread = col_count // row_count
    part = cols // col_count
    chunk = spread * part
    small = 2 * block // col_count
    sizes = (block, spread, part, col_count, small, tile_cols)
    place = jnp.stack([row_index, col_index]).astype(jnp.int32)
    tall = (cols, block)
    tile = (block, block)

    def chunks_of(values):
        split = values.reshape(tile_cols, spread, block // part, part, block)
        return split.transpose(0, 2, 1, 3, 4).reshape(col_count, chunk, block)

    def copies_of(value, count):
        return jnp.broadcast_to(value[None], (count,) + value.shape)

    def share(tall, little):
        got = exchange(copies_of(jnp.concatenate(tall + [little]), row_count), "row")
        wanted = []
        for index in range(len(tall)):
            piece = got[:, index * chunk : (index + 1) * chunk].reshape(row_count, spread, part, block)
            wanted.append(piece.transpose(1, 0, 2, 3).reshape(col_count, part, block))
        total = got[:, len(tall) * chunk :].sum(0)
        sends = [copies_of(tall[0], col_count), wanted[0], copies_of(total, col_count)] + wanted[1:]
        return exchange(jnp.concatenate(sends, axis=1), "col")

    current = matrix.reshape(rows, cols)

    own_col = current[:, :block]
    tile_ids = jnp.repeat(jnp.arange(tile_rows, dtype=jnp.int32) * row_count + row_index, block)[:, None]
    masked = jnp.where(tile_ids >= 1, own_col, 0.0)
    gram_part = dot(masked, masked, 0, 0)
    top_part = jnp.where(row_index == 1, own_col[:block], 0.0)
    stacked = jnp.concatenate([gram_part, top_part]).reshape(col_count, small, block)
    got = exchange(jnp.concatenate([chunks_of(own_col), stacked], axis=1), "col")
    next_chunk = got[1, :chunk]
    shared = share([got[0, :chunk]], got[0, chunk:])
    stacked = shared[:, chunk + part :].reshape(2 * block, block)
    even, odd = (shared[:, part * h : part * h + part].reshape(cols, block) for h in range(spread))
    panel_cols = shared[:, chunk : chunk + part].reshape(cols, block)

    for panel_index in range(2):
        last = panel_index == 1
        first = panel_index + 1
        send, even, odd, panel_cols, pivot_tile = launch(
            functools.partial(front_body, first=first, last=last, sizes=sizes),
            [(col_count, chunk + small, block), tall, tall, tall, tile],
            place, stacked, even, odd, panel_cols, current, scratch=tile,
        )
        (inverse_core,) = launch(newton_body, [tile], place, pivot_tile)
        mine = exchange(send, "col").sum(0)
        got = share([mine[:chunk]] + ([] if last else [next_chunk]), mine[chunk:])
        if last:
            (current,) = launch(
                functools.partial(final_body, sizes=sizes),
                [(rows * tile_cols, block)],
                place, current, got, inverse_core, even, odd, panel_cols, lines=tile_cols,
            )
            break
        send, core_block, companion_tile, next_cols = launch(
            functools.partial(middle_body, first=first, sizes=sizes),
            [(col_count, small, block), tile, tile, tall],
            place, got, inverse_core, panel_cols, pivot_tile,
        )
        shared = exchange(jnp.concatenate([copies_of(next_chunk, col_count), send], axis=1), "col")
        total = shared[:, chunk:].sum(0)
        stacked = exchange(copies_of(total, col_count), "col").reshape(2 * block, block)
        current, even, odd = launch(
            functools.partial(between_body, sizes=sizes),
            [(rows, cols), tall, tall],
            place, current, got, inverse_core, core_block, even, odd, panel_cols, companion_tile, pivot_tile, shared,
        )
        panel_cols = next_cols
    return current.reshape(matrix.shape)


def solution(mesh):
    in_specs = (P(None, "row", None, None, "col", None),)
    out_specs = P(None, "row", None, None, "col", None)
    return jax.shard_map(local, mesh=mesh, in_specs=in_specs, out_specs=out_specs, check_vma=False)
```

```python
import functools

import jax
import jax.numpy as jnp
from jax import lax
from jax.experimental import pallas as pl
from jax.experimental.pallas import tpu as pltpu
from jax.sharding import PartitionSpec as P

newton_sweeps = 8
pivot_group = 2


def dot(left_side, right_side, left_dim=1, right_dim=0):
    return lax.dot_general(
        left_side,
        right_side,
        (((left_dim,), (right_dim,)), ((), ())),
        precision=lax.Precision.HIGHEST,
        preferred_element_type=jnp.float32,
    )


def halves_of(values):
    high = values.astype(jnp.bfloat16)
    return high, (values - high.astype(jnp.float32)).astype(jnp.bfloat16)


def wide_dot(left_side, right_side, right_dim=0):
    left_high, left_low = halves_of(left_side)
    right_high, right_low = halves_of(right_side)

    def product(first, second):
        return lax.dot_general(
            first, second, (((1,), (right_dim,)), ((), ())), preferred_element_type=jnp.float32
        )

    return product(left_high, right_high) + (product(left_high, right_low) + product(left_low, right_high))


def newton_body(place, middle):
    identity = eye_of(middle.shape[0])
    power = identity - middle

    approx = identity + power
    for sweep_step in range(1, newton_sweeps):
        power = dot(power, power)
        approx = approx + dot(approx, power)
    return (approx,)


def exchange(chunks, axis):
    return lax.all_to_all(chunks, axis, 0, 0)


def eye_of(block):
    row = lax.broadcasted_iota(jnp.int32, (block, block), 0)
    lane = lax.broadcasted_iota(jnp.int32, (block, block), 1)
    return jnp.where(row == lane, 1.0, 0.0).astype(jnp.float32)


def factor_inverse(gram, scratch):
    block = gram.shape[0]
    tiles = block // 8
    shape = (8, block)
    lane = lax.broadcasted_iota(jnp.int32, shape, 1)
    sub = lax.broadcasted_iota(jnp.int32, shape, 0)
    left = [gram[8 * b : 8 * b + 8] for b in range(tiles)]
    right = [jnp.where(lane == sub + 8 * b, 1.0, 0.0).astype(jnp.float32) for b in range(tiles)]
    members = range(pivot_group)
    for start in range(0, block, pivot_group):
        home, top = start // 8, start % 8
        pivots = [jnp.broadcast_to(left[home][top + i : top + i + 1], shape) for i in members]
        shadows = [jnp.broadcast_to(right[home][top + i : top + i + 1], shape) for i in members]
        corner = [
            [
                jnp.broadcast_to(left[home][top + i : top + i + 1, start + m : start + m + 1], shape)
                for m in members
            ]
            for i in members
        ]
        inverse = []
        for i in members:
            root = lax.rsqrt(corner[i][i])
            inverse.append(root * root)
            scratch[start + i : start + i + 1, :] = (shadows[i] * root)[0:1]
            for j in range(i + 1, pivot_group):
                factor = corner[j][i] * inverse[i]
                pivots[j] = pivots[j] - factor * pivots[i]
                shadows[j] = shadows[j] - factor * shadows[i]
                for m in range(i + 1, pivot_group):
                    corner[j][m] = corner[j][m] - factor * corner[i][m]
        for b in range((start + pivot_group) // 8, tiles):
            column = [jnp.broadcast_to(left[b][:, start + i : start + i + 1], shape) for i in members]
            for i in members:
                factor = column[i] * inverse[i]
                for m in range(i + 1, pivot_group):
                    column[m] = column[m] - factor * corner[i][m]
                left[b] = left[b] - factor * pivots[i]
                right[b] = right[b] - factor * shadows[i]
    return scratch[...]


def launch(body, shapes, place, *operands, scratch=None, lines=None):
    outs = [jax.ShapeDtypeStruct(shape, jnp.float32) for shape in shapes]

    def kernel(*refs):
        extra = refs[len(refs) - 1 :] if scratch else ()
        inputs = refs[1 : 1 + len(operands)]
        results = body(refs[0], *[ref[...] for ref in inputs], *extra)
        for ref, value in zip(refs[1 + len(operands) : 1 + len(operands) + len(outs)], results, strict=True):
            if lines:
                width = value.shape[1] // lines
                for u in range(lines):
                    ref[pl.ds(u, value.shape[0], stride=lines), :] = value[:, u * width : (u + 1) * width]
            else:
                ref[...] = value

    vmem = pl.BlockSpec(memory_space=pltpu.VMEM)
    return pl.pallas_call(
        kernel,
        out_shape=outs,
        in_specs=[pl.BlockSpec(memory_space=pltpu.SMEM)] + [vmem] * len(operands),
        out_specs=[vmem] * len(outs),
        scratch_shapes=[pltpu.VMEM(scratch, jnp.float32)] if scratch else [],
    )(place, *operands)


def first_tile(values, block, change):
    return jnp.concatenate([change(values[:block]), values[block:]])


def keep_from(values, block, index, first):
    return first_tile(values, block, lambda tile: tile * jnp.where(index >= first, 1.0, 0.0))


def front_body(place, stacked, panel_even, panel_odd, panel_cols, current, scratch, *, first, last, sizes):
    block, spread, part, col_count, small, tile_cols = sizes
    identity = eye_of(block)
    lower_inverse = factor_inverse(stacked[:block], scratch)
    pivot_tile = identity + dot(stacked[block:], lower_inverse, 1, 1)

    def reflect(panel, index):
        q = dot(keep_from(panel, block, index, first), lower_inverse, 1, 1)
        return first_tile(q, block, lambda tile: tile + identity * jnp.where(index == first, 1.0, 0.0))

    cols = reflect(panel_cols, place[1])
    even = reflect(panel_even, place[0])
    odd = dot(panel_odd, lower_inverse, 1, 1)
    product = wide_dot(current, cols)
    tiles = [product[block * t : block * t + block] for t in range(spread * tile_cols)]
    sums = [jnp.concatenate(tiles[h::spread]) for h in range(spread)]
    cross = wide_dot(even.T, sums[0]) + wide_dot(odd.T, sums[1])
    if last:
        pivot_rows = jnp.zeros_like(cross)
    else:
        pivot_rows = tiles[0] * jnp.where(place[0] == first, 1.0, 0.0)
    little = jnp.concatenate([cross, pivot_rows]).reshape(col_count, small, block)
    send = jnp.concatenate([each.reshape(col_count, part, block) for each in sums] + [little], axis=1)
    return send, even, odd, cols, pivot_tile


def split_shared(got, start, sizes):
    block, spread, part, col_count, small, tile_cols = sizes
    pieces = [
        got[:, start + part * h : start + part * h + part].reshape(col_count * part, block) for h in range(spread + 1)
    ]
    return pieces[:spread], pieces[spread]


def companions(got, inverse_core, even, odd, cols, core_block, sizes):
    (w_even, w_odd), w_cols = split_shared(got, 0, sizes)
    pairs = ((w_even, even), (w_odd, odd), (w_cols, cols))
    return [dot(w, inverse_core, 1, 1) - 0.5 * dot(v, core_block) for w, v in pairs]


def middle_body(place, got, inverse_core, cols, pivot_tile, next_tile, *, first, sizes):
    block, spread, part, col_count, small, tile_cols = sizes
    little = got[:, (spread + 1) * part :].reshape(col_count * small, block)
    core_block = dot(dot(inverse_core, little[:block]), inverse_core, 1, 1)
    w_cols = split_shared(got, 0, sizes)[1]
    companion = dot(w_cols, inverse_core, 1, 1) - 0.5 * dot(cols, core_block)
    companion_tile = dot(little[block:], inverse_core, 1, 1) - 0.5 * dot(pivot_tile, core_block)
    panel = next_tile.T - (dot(cols, companion_tile, 1, 1) + dot(companion, pivot_tile, 1, 1))
    masked = keep_from(panel, block, place[1], first + 1)
    gram = dot(masked.T, masked)
    top = panel[:block] * jnp.where(place[1] == first + 1, 1.0, 0.0)
    send = jnp.concatenate([gram, top]).reshape(col_count, small, block)
    return send, core_block, companion_tile, panel


def update_tiles(current, even, odd, even_z, odd_z, cols, cols_z, sizes):
    block, spread, part, col_count, small, tile_cols = sizes
    right = jnp.concatenate([cols_z, cols], axis=1)
    lefts = [jnp.concatenate([even, even_z], axis=1), jnp.concatenate([odd, odd_z], axis=1)]
    pieces = [lefts[h][block * u : block * u + block] for u in range(tile_cols) for h in range(spread)]
    return current - wide_dot(jnp.concatenate(pieces), right, 1)


def between_body(place, current, got, inverse_core, core_block, even, odd, cols, companion_tile, pivot_tile, shared, *, sizes):
    block, spread, part, col_count, small, tile_cols = sizes
    even_z, odd_z, cols_z = companions(got, inverse_core, even, odd, cols, core_block, sizes)
    next_even, next_odd = (
        shared[:, part * h : part * h + part].reshape(col_count * part, block) for h in range(spread)
    )
    panels = [
        values - (dot(v, companion_tile, 1, 1) + dot(z, pivot_tile, 1, 1))
        for values, v, z in ((next_even, even, even_z), (next_odd, odd, odd_z))
    ]
    return update_tiles(current, even, odd, even_z, odd_z, cols, cols_z, sizes), panels[0], panels[1]


def final_body(place, current, got, inverse_core, even, odd, cols, *, sizes):
    block, spread, part, col_count, small, tile_cols = sizes
    cross = got[:, (spread + 1) * part :].reshape(col_count * small, block)[:block]
    core_block = dot(dot(inverse_core, cross), inverse_core, 1, 1)
    even_z, odd_z, cols_z = companions(got, inverse_core, even, odd, cols, core_block, sizes)
    return (update_tiles(current, even, odd, even_z, odd_z, cols, cols_z, sizes),)


def local(matrix):
    tile_rows, block, tile_cols = matrix.shape[0], matrix.shape[2], matrix.shape[3]
    rows, cols = tile_rows * block, tile_cols * block
    row_count, col_count = lax.axis_size("row"), lax.axis_size("col")
    row_index, col_index = lax.axis_index("row"), lax.axis_index("col")
    spread = col_count // row_count
    part = cols // col_count
    chunk = spread * part
    small = 2 * block // col_count
    sizes = (block, spread, part, col_count, small, tile_cols)
    place = jnp.stack([row_index, col_index]).astype(jnp.int32)
    tall = (cols, block)
    tile = (block, block)

    def chunks_of(values):
        split = values.reshape(tile_cols, spread, block // part, part, block)
        return split.transpose(0, 2, 1, 3, 4).reshape(col_count, chunk, block)

    def copies_of(value, count):
        return jnp.broadcast_to(value[None], (count,) + value.shape)

    def sum_rows(mine):
        return exchange(copies_of(mine, row_count), "row")

    def share(mine, got):
        wanted = got[:, :chunk].reshape(row_count, spread, part, block)
        wanted = wanted.transpose(1, 0, 2, 3).reshape(col_count, part, block)
        sends = [copies_of(mine[:chunk], col_count), wanted, copies_of(got[:, chunk:].sum(0), col_count)]
        return exchange(jnp.concatenate(sends, axis=1), "col")

    def hop(held, source, step):
        if step >= row_count:
            return held
        pairs = [((source + k) % row_count, (source + k + step) % row_count) for k in range(0, row_count, 2 * step)]
        return held + lax.ppermute(held, "row", pairs)

    def after(value, held):
        return lax.optimization_barrier((value, held))

    current = matrix.reshape(rows, cols)

    own_col = current[:, :block]
    tile_ids = jnp.repeat(jnp.arange(tile_rows, dtype=jnp.int32) * row_count + row_index, block)[:, None]
    masked = jnp.where(tile_ids >= 1, own_col, 0.0)
    gram_part = dot(masked, masked, 0, 0)
    top_part = jnp.where(row_index == 1, own_col[:block], 0.0)
    stacked = jnp.concatenate([gram_part, top_part]).reshape(col_count, small, block)
    got = exchange(jnp.concatenate([chunks_of(own_col), stacked], axis=1), "col")
    next_chunk = got[1, :chunk]
    mine = jnp.concatenate([got[0, :chunk], got[0, chunk:]])
    got, next_tile = after(sum_rows(mine), jnp.where(row_index == 1, current[:block], 0.0))
    shared, next_tile = after(share(mine, got), hop(next_tile, 1, 8))
    stacked = shared[:, chunk + part :].reshape(2 * block, block)
    even, odd = (shared[:, part * h : part * h + part].reshape(cols, block) for h in range(spread))
    panel_cols = shared[:, chunk : chunk + part].reshape(cols, block)

    for panel_index in range(2):
        last = panel_index == 1
        first = panel_index + 1
        send, even, odd, panel_cols, pivot_tile = launch(
            functools.partial(front_body, first=first, last=last, sizes=sizes),
            [(col_count, chunk + small, block), tall, tall, tall, tile],
            place, stacked, even, odd, panel_cols, current, scratch=tile,
        )
        (inverse_core,) = launch(newton_body, [tile], place, pivot_tile)
        if last:
            mine = exchange(send, "col").sum(0)
            got = share(mine, sum_rows(mine))
        else:
            send, next_tile = after(send, hop(next_tile, 1, 4))
            mine, next_tile = after(exchange(send, "col"), hop(next_tile, 1, 2))
            mine = mine.sum(0)
            got, next_tile = after(sum_rows(mine), next_tile)
            got, next_tile = after(share(mine, got), hop(next_tile, 1, 1))
        if last:
            (current,) = launch(
                functools.partial(final_body, sizes=sizes),
                [(rows * tile_cols, block)],
                place, current, got, inverse_core, even, odd, panel_cols, lines=tile_cols,
            )
            break
        send, core_block, companion_tile, next_cols = launch(
            functools.partial(middle_body, first=first, sizes=sizes),
            [(col_count, small, block), tile, tile, tall],
            place, got, inverse_core, panel_cols, pivot_tile, next_tile,
        )
        shared = exchange(jnp.concatenate([copies_of(next_chunk, col_count), send], axis=1), "col")
        total = shared[:, chunk:].sum(0)
        stacked = exchange(copies_of(total, col_count), "col").reshape(2 * block, block)
        current, even, odd = launch(
            functools.partial(between_body, sizes=sizes),
            [(rows, cols), tall, tall],
            place, current, got, inverse_core, core_block, even, odd, panel_cols, companion_tile, pivot_tile, shared,
        )
        panel_cols = next_cols
    return current.reshape(matrix.shape)


def solution(mesh):
    in_specs = (P(None, "row", None, None, "col", None),)
    out_specs = P(None, "row", None, None, "col", None)
    return jax.shard_map(local, mesh=mesh, in_specs=in_specs, out_specs=out_specs, check_vma=False)
```

```python
import functools

import jax
import jax.numpy as jnp
from jax import lax
from jax.experimental import pallas as pl
from jax.experimental.pallas import tpu as pltpu
from jax.sharding import PartitionSpec as P

newton_sweeps = 8
pivot_group = 8


def dot(left_side, right_side, left_dim=1, right_dim=0):
    return lax.dot_general(
        left_side,
        right_side,
        (((left_dim,), (right_dim,)), ((), ())),
        precision=lax.Precision.HIGHEST,
        preferred_element_type=jnp.float32,
    )


def halves_of(values):
    high = values.astype(jnp.bfloat16)
    return high, (values - high.astype(jnp.float32)).astype(jnp.bfloat16)


def wide_dot(left_side, right_side, right_dim=0):
    left_high, left_low = halves_of(left_side)
    right_high, right_low = halves_of(right_side)

    def product(first, second):
        return lax.dot_general(
            first, second, (((1,), (right_dim,)), ((), ())), preferred_element_type=jnp.float32
        )

    return product(left_high, right_high) + (product(left_high, right_low) + product(left_low, right_high))


def newton_body(place, middle):
    identity = eye_of(middle.shape[0])
    power = identity - middle

    approx = identity + power
    for sweep_step in range(1, newton_sweeps):
        power = dot(power, power)
        approx = approx + dot(approx, power)
    return (approx,)


def exchange(chunks, axis):
    return lax.all_to_all(chunks, axis, 0, 0)


def eye_of(block):
    row = lax.broadcasted_iota(jnp.int32, (block, block), 0)
    lane = lax.broadcasted_iota(jnp.int32, (block, block), 1)
    return jnp.where(row == lane, 1.0, 0.0).astype(jnp.float32)


def factor_inverse(gram, scratch):
    block = gram.shape[0]
    tiles = block // 8
    shape = (8, block)
    lane = lax.broadcasted_iota(jnp.int32, shape, 1)
    sub = lax.broadcasted_iota(jnp.int32, shape, 0)
    left = [gram[8 * b : 8 * b + 8] for b in range(tiles)]
    right = [jnp.where(lane == sub + 8 * b, 1.0, 0.0).astype(jnp.float32) for b in range(tiles)]
    members = range(pivot_group)
    for start in range(0, block, pivot_group):
        home, top = start // 8, start % 8
        pivots = [jnp.broadcast_to(left[home][top + i : top + i + 1], shape) for i in members]
        shadows = [jnp.broadcast_to(right[home][top + i : top + i + 1], shape) for i in members]
        corner = [
            [
                jnp.broadcast_to(left[home][top + i : top + i + 1, start + m : start + m + 1], shape)
                for m in members
            ]
            for i in members
        ]
        inverse = []
        for i in members:
            root = lax.rsqrt(corner[i][i])
            inverse.append(root * root)
            scratch[start + i : start + i + 1, :] = (shadows[i] * root)[0:1]
            for j in range(i + 1, pivot_group):
                factor = corner[j][i] * inverse[i]
                pivots[j] = pivots[j] - factor * pivots[i]
                shadows[j] = shadows[j] - factor * shadows[i]
                for m in range(i + 1, pivot_group):
                    corner[j][m] = corner[j][m] - factor * corner[i][m]
        for b in range((start + pivot_group) // 8, tiles):
            column = [jnp.broadcast_to(left[b][:, start + i : start + i + 1], shape) for i in members]
            for i in members:
                factor = column[i] * inverse[i]
                for m in range(i + 1, pivot_group):
                    column[m] = column[m] - factor * corner[i][m]
                left[b] = left[b] - factor * pivots[i]
                right[b] = right[b] - factor * shadows[i]
    return scratch[...]


def launch(body, shapes, place, *operands, scratch=None, lines=None, split=None):
    outs = [jax.ShapeDtypeStruct(shape, jnp.float32) for shape in shapes]

    def kernel(*refs):
        extra = refs[len(refs) - 1 :] if scratch else ()
        inputs = refs[1 : 1 + len(operands)]
        values = [ref[...] for ref in inputs[1 if split else 0 :]]
        if split:
            count = inputs[0].shape[0] // split
            runs = [inputs[0][pl.ds(u, count, stride=split), :] for u in range(split)]
            values.insert(0, jnp.concatenate(runs, axis=1))
        results = body(refs[0], *values, *extra)
        for ref, value in zip(refs[1 + len(operands) : 1 + len(operands) + len(outs)], results, strict=True):
            if lines:
                width = value.shape[1] // lines
                for u in range(lines):
                    ref[pl.ds(u, value.shape[0], stride=lines), :] = value[:, u * width : (u + 1) * width]
            else:
                ref[...] = value

    vmem = pl.BlockSpec(memory_space=pltpu.VMEM)
    return pl.pallas_call(
        kernel,
        out_shape=outs,
        in_specs=[pl.BlockSpec(memory_space=pltpu.SMEM)] + [vmem] * len(operands),
        out_specs=[vmem] * len(outs),
        scratch_shapes=[pltpu.VMEM(scratch, jnp.float32)] if scratch else [],
    )(place, *operands)


def first_tile(values, block, change):
    return jnp.concatenate([change(values[:block]), values[block:]])


def keep_from(values, block, index, first):
    return first_tile(values, block, lambda tile: tile * jnp.where(index >= first, 1.0, 0.0))


def front_body(place, stacked, panel_even, panel_odd, panel_cols, current, scratch, *, first, last, sizes):
    block, spread, part, col_count, small, tile_cols = sizes
    identity = eye_of(block)
    lower_inverse = factor_inverse(stacked[:block], scratch)
    pivot_tile = identity + dot(stacked[block:], lower_inverse, 1, 1)

    def reflect(panel, index):
        q = dot(keep_from(panel, block, index, first), lower_inverse, 1, 1)
        return first_tile(q, block, lambda tile: tile + identity * jnp.where(index == first, 1.0, 0.0))

    cols = reflect(panel_cols, place[1])
    even = reflect(panel_even, place[0])
    odd = dot(panel_odd, lower_inverse, 1, 1)
    product = wide_dot(current, cols)
    tiles = [product[block * t : block * t + block] for t in range(spread * tile_cols)]
    sums = [jnp.concatenate(tiles[h::spread]) for h in range(spread)]
    cross = wide_dot(even.T, sums[0]) + wide_dot(odd.T, sums[1])
    if last:
        pivot_rows = jnp.zeros_like(cross)
    else:
        pivot_rows = tiles[0] * jnp.where(place[0] == first, 1.0, 0.0)
    little = jnp.concatenate([cross, pivot_rows]).reshape(col_count, small, block)
    send = jnp.concatenate([each.reshape(col_count, part, block) for each in sums] + [little], axis=1)
    return send, even, odd, cols, pivot_tile


def pack_body(place, current, *, sizes):
    block, spread, part, col_count, small, tile_cols = sizes
    own = current[:, :block]
    masked = keep_from(own, block, place[0], 1)
    top = own[:block] * jnp.where(place[0] == 1, 1.0, 0.0)
    little = jnp.concatenate([dot(masked.T, masked), top]).reshape(col_count, small, block)
    tiles = [own[block * t : block * t + block] for t in range(spread * tile_cols)]
    sums = [jnp.concatenate(tiles[h::spread]) for h in range(spread)]
    return current, jnp.concatenate([each.reshape(col_count, part, block) for each in sums] + [little], axis=1)


def opening_body(place, shared, current, scratch, *, first, last, sizes):
    block, spread, part, col_count, small, tile_cols = sizes
    (even, odd), cols = split_shared(shared, 0, sizes)
    stacked = shared[:, (spread + 1) * part :].reshape(col_count * small, block)
    return front_body(place, stacked, even, odd, cols, current, scratch, first=first, last=last, sizes=sizes)


def split_shared(got, start, sizes):
    block, spread, part, col_count, small, tile_cols = sizes
    pieces = [
        got[:, start + part * h : start + part * h + part].reshape(col_count * part, block) for h in range(spread + 1)
    ]
    return pieces[:spread], pieces[spread]


def companions(got, inverse_core, even, odd, cols, core_block, sizes):
    (w_even, w_odd), w_cols = split_shared(got, 0, sizes)
    pairs = ((w_even, even), (w_odd, odd), (w_cols, cols))
    return [dot(w, inverse_core, 1, 1) - 0.5 * dot(v, core_block) for w, v in pairs]


def middle_body(place, got, inverse_core, cols, pivot_tile, next_tile, *, first, sizes):
    block, spread, part, col_count, small, tile_cols = sizes
    little = got[:, (spread + 1) * part :].reshape(col_count * small, block)
    core_block = dot(dot(inverse_core, little[:block]), inverse_core, 1, 1)
    w_cols = split_shared(got, 0, sizes)[1]
    companion = dot(w_cols, inverse_core, 1, 1) - 0.5 * dot(cols, core_block)
    companion_tile = dot(little[block:], inverse_core, 1, 1) - 0.5 * dot(pivot_tile, core_block)
    panel = next_tile.T - (dot(cols, companion_tile, 1, 1) + dot(companion, pivot_tile, 1, 1))
    masked = keep_from(panel, block, place[1], first + 1)
    gram = dot(masked.T, masked)
    top = panel[:block] * jnp.where(place[1] == first + 1, 1.0, 0.0)
    send = jnp.concatenate([gram, top]).reshape(col_count, small, block)
    return send, core_block, companion_tile, panel


def update_tiles(current, even, odd, even_z, odd_z, cols, cols_z, sizes):
    block, spread, part, col_count, small, tile_cols = sizes
    right = jnp.concatenate([cols_z, cols], axis=1)
    lefts = [jnp.concatenate([even, even_z], axis=1), jnp.concatenate([odd, odd_z], axis=1)]
    pieces = [lefts[h][block * u : block * u + block] for u in range(tile_cols) for h in range(spread)]
    return current - wide_dot(jnp.concatenate(pieces), right, 1)


def between_body(place, current, got, inverse_core, core_block, even, odd, cols, companion_tile, pivot_tile, shared, *, sizes):
    block, spread, part, col_count, small, tile_cols = sizes
    even_z, odd_z, cols_z = companions(got, inverse_core, even, odd, cols, core_block, sizes)
    next_even, next_odd = (
        shared[:, part * h : part * h + part].reshape(col_count * part, block) for h in range(spread)
    )
    panels = [
        values - (dot(v, companion_tile, 1, 1) + dot(z, pivot_tile, 1, 1))
        for values, v, z in ((next_even, even, even_z), (next_odd, odd, odd_z))
    ]
    return update_tiles(current, even, odd, even_z, odd_z, cols, cols_z, sizes), panels[0], panels[1]


def final_body(place, current, got, inverse_core, even, odd, cols, *, sizes):
    block, spread, part, col_count, small, tile_cols = sizes
    cross = got[:, (spread + 1) * part :].reshape(col_count * small, block)[:block]
    core_block = dot(dot(inverse_core, cross), inverse_core, 1, 1)
    even_z, odd_z, cols_z = companions(got, inverse_core, even, odd, cols, core_block, sizes)
    return (update_tiles(current, even, odd, even_z, odd_z, cols, cols_z, sizes),)


def local(matrix):
    tile_rows, block, tile_cols = matrix.shape[0], matrix.shape[2], matrix.shape[3]
    rows, cols = tile_rows * block, tile_cols * block
    row_count, col_count = lax.axis_size("row"), lax.axis_size("col")
    row_index, col_index = lax.axis_index("row"), lax.axis_index("col")
    spread = col_count // row_count
    part = cols // col_count
    chunk = spread * part
    small = 2 * block // col_count
    sizes = (block, spread, part, col_count, small, tile_cols)
    place = jnp.stack([row_index, col_index]).astype(jnp.int32)
    tall = (cols, block)
    tile = (block, block)

    def copies_of(value, count):
        return jnp.broadcast_to(value[None], (count,) + value.shape)

    def sum_rows(mine):
        return exchange(copies_of(mine, row_count), "row")

    def share(mine, got):
        wanted = got[:, :chunk].reshape(row_count, spread, part, block)
        wanted = wanted.transpose(1, 0, 2, 3).reshape(col_count, part, block)
        sends = [copies_of(mine[:chunk], col_count), wanted, copies_of(got[:, chunk:].sum(0), col_count)]
        return exchange(jnp.concatenate(sends, axis=1), "col")

    def hop(held, source, step):
        if step >= row_count:
            return held
        pairs = [((source + k) % row_count, (source + k + step) % row_count) for k in range(0, row_count, 2 * step)]
        return held + lax.ppermute(held, "row", pairs)

    def after(value, held):
        return lax.optimization_barrier((value, held))

    current, send = launch(
        functools.partial(pack_body, sizes=sizes),
        [(rows, cols), (col_count, chunk + small, block)],
        place, matrix.reshape(rows * tile_cols, block), split=tile_cols,
    )
    got = exchange(send, "col")
    next_chunk = got[1, :chunk]
    mine = jnp.concatenate([got[0, :chunk], got[0, chunk:]])
    got, next_tile = after(sum_rows(mine), jnp.where(row_index == 1, current[:block], 0.0))
    shared, next_tile = after(share(mine, got), hop(next_tile, 1, 8))
    opening = [shared]

    for panel_index in range(2):
        last = panel_index == 1
        first = panel_index + 1
        send, even, odd, panel_cols, pivot_tile = launch(
            functools.partial(front_body if last else opening_body, first=first, last=last, sizes=sizes),
            [(col_count, chunk + small, block), tall, tall, tall, tile],
            place, *opening, current, scratch=tile,
        )
        (inverse_core,) = launch(newton_body, [tile], place, pivot_tile)
        if last:
            mine = exchange(send, "col").sum(0)
            got = share(mine, sum_rows(mine))
        else:
            send, next_tile = after(send, hop(next_tile, 1, 4))
            mine, next_tile = after(exchange(send, "col"), hop(next_tile, 1, 2))
            mine = mine.sum(0)
            got, next_tile = after(sum_rows(mine), next_tile)
            got, next_tile = after(share(mine, got), hop(next_tile, 1, 1))
        if last:
            (current,) = launch(
                functools.partial(final_body, sizes=sizes),
                [(rows * tile_cols, block)],
                place, current, got, inverse_core, even, odd, panel_cols, lines=tile_cols,
            )
            break
        send, core_block, companion_tile, next_cols = launch(
            functools.partial(middle_body, first=first, sizes=sizes),
            [(col_count, small, block), tile, tile, tall],
            place, got, inverse_core, panel_cols, pivot_tile, next_tile,
        )
        shared = exchange(jnp.concatenate([copies_of(next_chunk, col_count), send], axis=1), "col")
        total = shared[:, chunk:].sum(0)
        stacked = exchange(copies_of(total, col_count), "col").reshape(2 * block, block)
        current, even, odd = launch(
            functools.partial(between_body, sizes=sizes),
            [(rows, cols), tall, tall],
            place, current, got, inverse_core, core_block, even, odd, panel_cols, companion_tile, pivot_tile, shared,
        )
        opening = [stacked, even, odd, next_cols]
    return current.reshape(matrix.shape)


def solution(mesh):
    in_specs = (P(None, "row", None, None, "col", None),)
    out_specs = P(None, "row", None, None, "col", None)
    return jax.shard_map(local, mesh=mesh, in_specs=in_specs, out_specs=out_specs, check_vma=False)
```
